32 devices in a mesh: seq: 8 (over y, x, core), tp: 4 (over z).
Axes of the slice: x: 2, y: 2, z: 4, core: 2. Of those that a mesh axis runs over, the one named last changes fastest.
Arguments:
- queries: bfloat16 [4096, 4096], P('seq', 'tp'), may hold values from -6 to 6
- token_keys: bfloat16 [4096, 4096], P('seq', 'tp'), may hold values from -6 to 6
- token_values: bfloat16 [4096, 4096], P('seq', 'tp'), may hold values from -6 to 6
- out_weight: bfloat16 [4096, 4096], P('tp'), may hold values from -0.09375 to 0.09375
- out_grad: bfloat16 [4096, 4096], P('seq'), may hold values from -6 to 6
Outputs:
- layer_out: bfloat16 [4096, 4096], P('seq', 'tp')
- query_grad: bfloat16 [4096, 4096], P('seq', 'tp')
- key_grad: bfloat16 [4096, 4096], P('seq', 'tp')
- value_grad: bfloat16 [4096, 4096], P('seq', 'tp')
- weight_grad: float32 [4096, 4096], P('tp', 'seq')
The draws below stay inside these ranges and needn't reach their ends.
All inputs are finite; a program needn't handle non-finite values.
Results may differ from the reference program's by a relative error of at most 0.024.
Values may be sent and summed in bfloat16 or wider, within the bound.
A program may use at most 256 MiB of HBM per device.

```python
import math
import jax
import jax.numpy as jnp
from jax import lax

HEADS = 32
DH = 128
D = 4096
TOK_DEV = 512
FB = 128
P1 = 16
P2 = 256
HD = 4096
TOKENS = 4096
N_SEQ = 8


def base_field(field_key):
    return jax.random.truncated_normal(field_key, -6.0, 6.0, (TOKENS, HEADS * DH), jnp.float32)


def draw_queries(key, part):
    field = base_field(jax.random.fold_in(key, 101))
    return field.astype(jnp.bfloat16)


def draw_token_keys(key, part):
    field = base_field(jax.random.fold_in(key, 202))
    return field.astype(jnp.bfloat16)


def raised(entries, rng, source, target, blocks, factor):
    owner, partner = [(jnp.arange(entries.shape[dim]) // (entries.shape[dim] // blocks)).reshape([-1 if axis == dim else 1 for axis in range(entries.ndim)]) for dim in (source, target)]
    chosen = jax.random.permutation(rng, blocks)[partner]
    strong = (owner == chosen) | (owner == (partner + blocks // 2) % blocks)
    return jnp.where(strong, factor * entries, entries)


def levels(own_key, shape, cuts, low, high):
    factor_of, own = 1.0, jax.random.fold_in(own_key, 6)
    for axis_at, parts in cuts:
        draws = jnp.exp(jax.random.uniform(jax.random.fold_in(own, axis_at), (parts,), jnp.float32, low / len(cuts), high / len(cuts)))
        factor_of = factor_of * jnp.repeat(draws, shape[axis_at] // parts).reshape([-1 if axis == axis_at else 1 for axis in range(len(shape))])
    return factor_of


def noise(key, shape, width, bound, shards=(), kind=jnp.bfloat16):
    values = jax.random.normal(key, shape, jnp.float32) * width
    if len(shards) > 0:
        values = levels(key, shape, shards, -0.22, 0.18) * values
    return jnp.clip(values, min=-bound, max=bound).astype(kind)


def bell_draw_with(stream_key, shape, width, most, cuts, heavy, kind=jnp.bfloat16):
    drawn = width * jax.random.normal(stream_key, shape, jnp.float32)
    if cuts:
        drawn = drawn * levels(stream_key, shape, cuts, -0.22, 0.18)
    return jnp.clip(raised(drawn, jax.random.fold_in(stream_key, 3), *heavy), -most, most).astype(kind)


def setup_inputs(seed: int = 0) -> dict:
    streams_of = jax.random.split(jax.random.key(seed), 6)
    return {
        "queries": draw_queries(jax.random.fold_in(streams_of[5], 71), 0),
        "token_keys": draw_token_keys(jax.random.fold_in(streams_of[5], 71), 0),
        "token_values": noise(streams_of[2], (TOKENS, HD), 1.0, 6.0, ((0, 8), (1, 4))),
        "out_weight": noise(streams_of[3], (HD, D), HD ** -0.5, 0.09375, ((0, 4),)),
        "out_grad": bell_draw_with(streams_of[4], (TOKENS, D), 1.0, 6.0, ((0, 8),), (0, 1, 8, 2.0)),
    }


def product(form, left, right):
    return jnp.einsum(form, left.astype(jnp.float32), right.astype(jnp.float32))

def pooled(stacked, group_size):
    count_rows = stacked.shape[1] // group_size
    summed = stacked.astype(jnp.float32).reshape(stacked.shape[0], count_rows, group_size, stacked.shape[2]).sum(axis=2)
    return (summed / group_size).astype(jnp.bfloat16)

def expand_rows(grad_parts, group_size):
    shaped = jnp.broadcast_to(grad_parts[:, :, None, :] / group_size, (grad_parts.shape[0], grad_parts.shape[1], group_size, grad_parts.shape[2]))
    return shaped.reshape(grad_parts.shape[0], grad_parts.shape[1] * group_size, grad_parts.shape[2])

def fold_windows(window_grad, blocks):
    leading = window_grad.shape[0]
    split_grad = window_grad.reshape(leading, blocks, 3, FB, -1)
    first_part = jnp.pad(split_grad[:, :, 0], ((0, 0), (0, 2), (0, 0), (0, 0)))
    middle = jnp.pad(split_grad[:, :, 1], ((0, 0), (1, 1), (0, 0), (0, 0)))
    last_part = jnp.pad(split_grad[:, :, 2], ((0, 0), (2, 0), (0, 0), (0, 0)))
    return (first_part + middle + last_part).reshape(leading, (blocks + 2) * FB, -1)

def attend(query_rows, extended, extended_pooled, coarse_rows, grad_rows, position, seq_count):
    tokens_here, features = query_rows.shape
    head_count = features // DH
    blocks = tokens_here // FB
    pooled_rows = extended_pooled.shape[1] // 3
    coarse_count = coarse_rows.shape[1]
    scaling = 1.0 / math.sqrt(DH)
    query_blocks = query_rows.reshape(blocks, FB, head_count, DH)
    token_blocks = extended.reshape(2, blocks + 2, FB, head_count, DH)
    windows = jnp.concatenate([token_blocks[:, offset:offset + blocks] for offset in range(3)], axis=2)
    coarse_all = jnp.concatenate([extended_pooled, coarse_rows], axis=1).reshape(2, 3 * pooled_rows + coarse_count, head_count, DH)
    block_ids = jnp.arange(blocks, dtype=jnp.int32)[:, None]
    window_rows = block_ids * FB + jnp.arange(3 * FB, dtype=jnp.int32)[None, :]
    first_dev = position == 0
    last_dev = position == seq_count - 1
    fine_mask = jnp.logical_not(jnp.logical_or(jnp.logical_and(window_rows < FB, first_dev), jnp.logical_and(window_rows >= tokens_here + FB, last_dev)))
    group_ids = jnp.arange(3 * pooled_rows, dtype=jnp.int32)
    group_dev = group_ids // pooled_rows
    present = jnp.logical_not(jnp.logical_or(jnp.logical_and(group_dev == 0, first_dev), jnp.logical_and(group_dev == 2, last_dev)))
    distance = group_ids[None, :] * P1 // FB - blocks - block_ids
    near_mask = jnp.logical_and(present[None, :], jnp.abs(distance) > 1)
    coarse_dev = jnp.arange(coarse_count, dtype=jnp.int32) * P2 // tokens_here
    far_mask = jnp.abs(coarse_dev - position) > 1
    coarse_mask = jnp.concatenate([near_mask, jnp.broadcast_to(far_mask[None, :], (blocks, coarse_count))], axis=1)
    level_bias = jnp.concatenate([jnp.full((3 * pooled_rows,), math.log(P1), jnp.float32), jnp.full((coarse_count,), math.log(P2), jnp.float32)])
    fine_scores = jnp.where(fine_mask[None, :, None, :], product('bqhd,bkhd->hbqk', query_blocks, windows[0]) * scaling, -jnp.inf)
    coarse_scores = jnp.where(coarse_mask[None, :, None, :], product('bqhd,khd->hbqk', query_blocks, coarse_all[0]) * scaling + level_bias, -jnp.inf)
    row_peak = jnp.maximum(fine_scores.max(axis=-1), coarse_scores.max(axis=-1))
    row_total = jnp.exp(fine_scores - row_peak[..., None]).sum(axis=-1) + jnp.exp(coarse_scores - row_peak[..., None]).sum(axis=-1)
    log_total = row_peak + jnp.log(row_total)
    fine_prob = jnp.exp(fine_scores - log_total[..., None])
    coarse_prob = jnp.exp(coarse_scores - log_total[..., None])
    fine_round = fine_prob.astype(jnp.bfloat16)
    coarse_round = coarse_prob.astype(jnp.bfloat16)
    attention = (product('hbqk,bkhd->bqhd', fine_round, windows[1]) + product('hbqk,khd->bqhd', coarse_round, coarse_all[1])).astype(jnp.bfloat16)
    grad_blocks = grad_rows.reshape(blocks, FB, head_count, DH)
    row_delta = product('bqhd,bqhd->hbq', grad_blocks, attention)
    fine_ds = (fine_prob * (product('bqhd,bkhd->hbqk', grad_blocks, windows[1]) - row_delta[..., None])).astype(jnp.bfloat16)
    coarse_ds = (coarse_prob * (product('bqhd,khd->hbqk', grad_blocks, coarse_all[1]) - row_delta[..., None])).astype(jnp.bfloat16)
    query_grad = ((product('hbqk,bkhd->bqhd', fine_ds, windows[0]) + product('hbqk,khd->bqhd', coarse_ds, coarse_all[0])) * scaling).astype(jnp.bfloat16)
    window_grad = jnp.stack([product('hbqk,bqhd->bkhd', fine_ds, query_blocks) * scaling, product('hbqk,bqhd->bkhd', fine_round, grad_blocks)])
    coarse_grad = jnp.stack([product('hbqk,bqhd->khd', coarse_ds, query_blocks) * scaling, product('hbqk,bqhd->khd', coarse_round, grad_blocks)])
    coarse_grad = coarse_grad.reshape(2, 3 * pooled_rows + coarse_count, features)
    extended_grad = fold_windows(window_grad.reshape(2, blocks, 3 * FB, features), blocks)
    return (attention.reshape(tokens_here, features), query_grad.reshape(tokens_here, features), extended_grad, coarse_grad[:, :3 * pooled_rows], coarse_grad[:, 3 * pooled_rows:])

def reference(queries, token_keys, token_values, out_weight, out_grad):
    features = HEADS * DH
    pooled_rows = TOK_DEV // P1
    stacked = jnp.stack([token_keys, token_values])
    fine_pad = jnp.pad(stacked, ((0, 0), (FB, FB), (0, 0)))
    near_rows = pooled(stacked, P1)
    near_pad = jnp.pad(near_rows, ((0, 0), (pooled_rows, pooled_rows), (0, 0)))
    far_rows = pooled(stacked, P2)
    attn_grad = lax.dot_general(out_grad, out_weight, (((1,), (1,)), ((), ())), preferred_element_type=jnp.float32).astype(jnp.bfloat16)
    anchor = jnp.zeros((), jnp.int32)

    def one_block(position):
        row_start = (position * TOK_DEV).astype(jnp.int32)
        query_rows = lax.dynamic_slice(queries, (row_start, anchor), (TOK_DEV, features))
        extended = lax.dynamic_slice(fine_pad, (anchor, row_start, anchor), (2, TOK_DEV + 2 * FB, features))
        extended_pooled = lax.dynamic_slice(near_pad, (anchor, (position * pooled_rows).astype(jnp.int32), anchor), (2, 3 * pooled_rows, features))
        grad_rows = lax.dynamic_slice(attn_grad, (row_start, anchor), (TOK_DEV, features))
        return attend(query_rows, extended, extended_pooled, far_rows, grad_rows, position, N_SEQ)
    attention, query_grad, window_grad, near_grad, far_grad = lax.map(one_block, jnp.arange(N_SEQ, dtype=jnp.int32))
    empty_fine = jnp.zeros_like(window_grad[:1, :, :FB])
    from_right = jnp.concatenate([window_grad[1:, :, :FB], empty_fine], axis=0)
    from_left = jnp.concatenate([empty_fine, window_grad[:-1, :, TOK_DEV + FB:]], axis=0)
    fine_total = window_grad[:, :, FB:FB + TOK_DEV] + jnp.pad(from_left, ((0, 0), (0, 0), (0, TOK_DEV - FB), (0, 0))) + jnp.pad(from_right, ((0, 0), (0, 0), (TOK_DEV - FB, 0), (0, 0)))
    empty_near = jnp.zeros_like(near_grad[:1, :, :pooled_rows])
    near_total = near_grad[:, :, pooled_rows:2 * pooled_rows] + jnp.concatenate([near_grad[1:, :, :pooled_rows], empty_near], axis=0) + jnp.concatenate([empty_near, near_grad[:-1, :, 2 * pooled_rows:]], axis=0)
    far_total = far_grad.sum(axis=0)
    fine_total = fine_total.transpose(1, 0, 2, 3).reshape(2, TOKENS, features)
    near_total = near_total.transpose(1, 0, 2, 3).reshape(2, TOKENS // P1, features)
    grand = fine_total + expand_rows(near_total, P1) + expand_rows(far_total, P2)
    attention = attention.reshape(TOKENS, features)
    query_grad = query_grad.reshape(TOKENS, features)
    layer_out = jnp.dot(attention, out_weight, preferred_element_type=jnp.float32).astype(jnp.bfloat16)
    weight_grad = jnp.dot(attention.T, out_grad, preferred_element_type=jnp.float32) * (1.0 / math.sqrt(TOKENS))
    return (layer_out, query_grad, grand[0].astype(jnp.bfloat16), grand[1].astype(jnp.bfloat16), weight_grad)
```

```python
import math

import jax
import jax.numpy as jnp
from jax import lax
from jax.experimental import pallas as pl
from jax.experimental.pallas import tpu as pltpu
from jax.sharding import PartitionSpec as P

DH = 128
FB = 128
P1 = 16
P2 = 256
NEG = -1e30


def contract(left, right, dim_left, dim_right):
    return lax.dot_general(
        left,
        right,
        (((dim_left,), (dim_right,)), ((), ())),
        preferred_element_type=jnp.float32,
    )


def expanded(rows, size):
    count, width = rows.shape
    return jnp.broadcast_to((rows / size)[:, None, :], (count, size, width)).reshape(
        count * size, width
    )


def pooled_rows_of(cells, group_size):
    rows, features = cells.shape
    summed = cells.astype(jnp.float32).reshape(rows // group_size, group_size, features).sum(axis=1)
    return (summed / group_size).astype(jnp.bfloat16)


def attend_kernel(
    bias_ref, q_ref, g_ref, k_ref, v_ref, left_ref, right_ref, near_ref, far_ref,
    att_ref, dq_ref, base_ref, to_left_ref, to_right_ref, dfar_ref,
):
    tokens = q_ref.shape[0]
    blocks = tokens // FB
    near = near_ref.shape[1]
    far = far_ref.shape[1]
    coarse = bias_ref.shape[1] - 3 * FB
    padding = coarse - 3 * near - far
    scaling = 1.0 / math.sqrt(DH)

    def pieces(own_ref, kind):
        fine = [left_ref[kind, :FB, :]]
        fine += [own_ref[i * FB : (i + 1) * FB, :] for i in range(blocks)]
        fine += [right_ref[kind, :FB, :]]
        rows = [left_ref[kind, FB:, :], near_ref[kind], right_ref[kind, FB:, :], far_ref[kind]]
        if padding:
            rows.append(jnp.zeros((padding, DH), jnp.bfloat16))
        return fine, jnp.concatenate(rows, axis=0)

    fine_keys, coarse_keys = pieces(k_ref, 0)
    fine_values, coarse_values = pieces(v_ref, 1)
    fine_grads = [[None] * (blocks + 2), [None] * (blocks + 2)]
    coarse_grads = [None, None]

    def add(old, new):
        return new if old is None else old + new

    for b in range(blocks):
        at = slice(b * FB, (b + 1) * FB)
        keys = jnp.concatenate(fine_keys[b : b + 3] + [coarse_keys], axis=0)
        values = jnp.concatenate(fine_values[b : b + 3] + [coarse_values], axis=0)
        query = q_ref[at, :]
        grad = g_ref[at, :]
        scores = contract(keys, query, 1, 1) * scaling + bias_ref[b]
        peak = jnp.max(scores, axis=0, keepdims=True)
        raw = jnp.exp(scores - peak)
        prob = raw * (1.0 / jnp.sum(raw, axis=0, keepdims=True))
        rounded = prob.astype(jnp.bfloat16)
        att = contract(values, rounded, 0, 0).T.astype(jnp.bfloat16)
        att_ref[at, :] = att
        moved = (grad.astype(jnp.float32) * att.astype(jnp.float32)).T
        delta = jnp.sum(moved, axis=0, keepdims=True)
        ds = (prob * (contract(values, grad, 1, 1) - delta)).astype(jnp.bfloat16)
        dq_ref[at, :] = (contract(keys, ds, 0, 0) * scaling).T.astype(jnp.bfloat16)
        for kind, part in enumerate(
            (contract(ds, query, 1, 0) * scaling, contract(rounded, grad, 1, 0))
        ):
            for i in range(3):
                fine_grads[kind][b + i] = add(
                    fine_grads[kind][b + i], part[i * FB : (i + 1) * FB]
                )
            coarse_grads[kind] = add(coarse_grads[kind], part[3 * FB :])
    for kind in range(2):
        fine, rows = fine_grads[kind], coarse_grads[kind]
        to_left_ref[kind, :FB, :] = fine[0]
        to_left_ref[kind, FB:, :] = rows[:near]
        to_right_ref[kind, :FB, :] = fine[blocks + 1]
        to_right_ref[kind, FB:, :] = rows[2 * near : 3 * near]
        dfar_ref[kind] = rows[3 * near : 3 * near + far]
        own = rows[near : 2 * near]
        groups = FB // P1
        for i in range(blocks):
            base_ref[kind, i * FB : (i + 1) * FB, :] = fine[i + 1] + expanded(
                own[i * groups : (i + 1) * groups], P1
            )


def attend(queries, grads, keys, values, left, right, near_rows, far_rows, bias):
    tokens, features = queries.shape
    heads = features // DH
    near = near_rows.shape[1]
    far = far_rows.shape[1]
    reach = FB + near

    def flat(rows):
        return pl.BlockSpec((rows, DH), lambda h: (0, h))

    def pair(rows):
        return pl.BlockSpec((2, rows, DH), lambda h: (0, 0, h))

    shape = jax.ShapeDtypeStruct
    scores = tokens * bias.shape[1] * heads
    return pl.pallas_call(
        attend_kernel,
        grid=(heads,),
        in_specs=[
            pl.BlockSpec(bias.shape, lambda h: (0, 0, 0)),
            flat(tokens), flat(tokens), flat(tokens), flat(tokens),
            pair(reach), pair(reach), pair(near), pair(far),
        ],
        out_specs=[
            flat(tokens), flat(tokens), pair(tokens), pair(reach), pair(reach), pair(far),
        ],
        out_shape=[
            shape((tokens, features), jnp.bfloat16),
            shape((tokens, features), jnp.bfloat16),
            shape((2, tokens, features), jnp.float32),
            shape((2, reach, features), jnp.float32),
            shape((2, reach, features), jnp.float32),
            shape((2, far, features), jnp.float32),
        ],
        cost_estimate=pl.CostEstimate(
            flops=12 * scores * DH, bytes_accessed=24 * tokens * features, transcendentals=scores
        ),
    )(bias, queries, grads, keys, values, left, right, near_rows, far_rows)


def combine_kernel(base_ref, left_ref, right_ref, far_ref, dk_ref, dv_ref):
    tokens = base_ref.shape[1]
    for kind, out_ref in enumerate((dk_ref, dv_ref)):
        near = left_ref[kind, FB:, :] + right_ref[kind, FB:, :]
        total = base_ref[kind] + expanded(near, P1) + expanded(far_ref[kind], P2)
        pieces = [total[i * FB : (i + 1) * FB] for i in range(tokens // FB)]
        pieces[0] = pieces[0] + left_ref[kind, :FB, :]
        pieces[-1] = pieces[-1] + right_ref[kind, :FB, :]
        for i, piece in enumerate(pieces):
            out_ref[i * FB : (i + 1) * FB, :] = piece.astype(jnp.bfloat16)


def combine(base, left, right, far):
    _, tokens, features = base.shape
    width = 256

    def pair(cells):
        return pl.BlockSpec((2, cells.shape[1], width), lambda h: (0, 0, h))

    flat = pl.BlockSpec((tokens, width), lambda h: (0, h))
    out = jax.ShapeDtypeStruct((tokens, features), jnp.bfloat16)
    return pl.pallas_call(
        combine_kernel,
        grid=(features // width,),
        in_specs=[pair(base), pair(left), pair(right), pair(far)],
        out_specs=[flat, flat],
        out_shape=[out, out],
        cost_estimate=pl.CostEstimate(
            flops=8 * tokens * features, bytes_accessed=14 * tokens * features, transcendentals=0
        ),
    )(base, left, right, far)


def key_bias(tokens, near, far, position, seq_count):
    blocks = tokens // FB
    block_ids = jnp.arange(blocks, dtype=jnp.int32)[:, None]
    first_dev = position == 0
    last_dev = position == seq_count - 1
    window_rows = block_ids * FB + jnp.arange(3 * FB, dtype=jnp.int32)[None, :]
    absent = jnp.logical_or(
        jnp.logical_and(window_rows < FB, first_dev),
        jnp.logical_and(window_rows >= tokens + FB, last_dev),
    )
    fine = jnp.where(absent, NEG, 0.0)
    group_ids = jnp.arange(3 * near, dtype=jnp.int32)
    group_dev = group_ids // near
    present = jnp.logical_not(
        jnp.logical_or(
            jnp.logical_and(group_dev == 0, first_dev), jnp.logical_and(group_dev == 2, last_dev)
        )
    )
    distance = group_ids[None, :] * P1 // FB - blocks - block_ids
    near_seen = jnp.logical_and(present[None, :], jnp.abs(distance) > 1)
    near_bias = jnp.where(near_seen, math.log(P1), NEG)
    far_dev = jnp.arange(far, dtype=jnp.int32) * P2 // tokens
    far_bias = jnp.where(jnp.abs(far_dev - position) > 1, math.log(P2), NEG)
    padding = -(3 * near + far) % FB
    row = jnp.concatenate(
        [
            fine,
            near_bias,
            jnp.broadcast_to(far_bias[None, :], (blocks, far)),
            jnp.full((blocks, padding), NEG),
        ],
        axis=1,
    ).astype(jnp.float32)
    return jnp.broadcast_to(row[:, :, None], row.shape + (FB,))


def shards(queries, token_keys, token_values, out_weight, out_grad):
    position = lax.axis_index("seq")
    seq_count = lax.axis_size("seq")
    tokens, features = queries.shape
    grad_scale = 1.0 / math.sqrt(tokens * seq_count)
    near = tokens // P1
    rightward = [(i, i + 1) for i in range(seq_count - 1)]
    leftward = [(i + 1, i) for i in range(seq_count - 1)]
    near_rows = jnp.stack([pooled_rows_of(token_keys, P1), pooled_rows_of(token_values, P1)])
    far_rows = jnp.stack([pooled_rows_of(token_keys, P2), pooled_rows_of(token_values, P2)])

    def packet(start):
        edges = jnp.stack([token_keys[start : start + FB], token_values[start : start + FB]])
        return jnp.concatenate([edges, near_rows], axis=1)

    far_all = lax.all_gather(far_rows, "seq", axis=1, tiled=True)
    left = lax.ppermute(packet(tokens - FB), "seq", rightward)
    right = lax.ppermute(packet(0), "seq", leftward)
    attn_grad = lax.dot_general(
        out_grad, out_weight, (((1,), (1,)), ((), ())), preferred_element_type=jnp.float32
    ).astype(jnp.bfloat16)
    columns = lax.all_to_all(out_grad, "seq", split_axis=1, concat_axis=0, tiled=True)
    bias = key_bias(tokens, near, far_all.shape[1], position, seq_count)
    attention, query_grad, base, to_left, to_right, far_grad = attend(
        queries, attn_grad, token_keys, token_values, left, right, near_rows, far_all, bias
    )
    gathered = lax.all_gather(attention, "seq", axis=0, tiled=True)
    left_back = lax.ppermute(to_right, "seq", rightward)
    right_back = lax.ppermute(to_left, "seq", leftward)
    far_total = lax.psum_scatter(far_grad, "seq", scatter_dimension=1, tiled=True)
    head_part = jnp.dot(attention, out_weight, preferred_element_type=jnp.float32)
    layer_out = lax.psum_scatter(head_part, "tp", scatter_dimension=1, tiled=True).astype(
        jnp.bfloat16
    )
    weight_sum = contract(gathered, columns, 0, 0)
    key_grad, value_grad = combine(base, left_back, right_back, far_total)
    return layer_out, query_grad, key_grad, value_grad, weight_sum * grad_scale


def solution(mesh):
    return jax.shard_map(
        shards,
        mesh=mesh,
        in_specs=(P("seq", "tp"), P("seq", "tp"), P("seq", "tp"), P("tp", None), P("seq", None)),
        out_specs=(P("seq", "tp"), P("seq", "tp"), P("seq", "tp"), P("seq", "tp"), P("tp", "seq")),
        check_vma=False,
    )
```
